512 devices in a mesh: row: 64 (over z, y), col: 8 (over x, core).
Axes of the slice: x: 4, y: 8, z: 8, core: 2. Of those that a mesh axis runs over, the one named last changes fastest.
Arguments:
- dinv0: bfloat16 [65536, 4096], P('row', 'col'), as said below
- dinv1: bfloat16 [32768, 4096], P('row', 'col'), as said below
- dinv2: bfloat16 [16384, 4096], P('row', 'col'), as said below
- offdiag0: bfloat16 [65536, 4096], P('row', 'col'), may hold values from -0.0625 to 0.0625
- offdiag1: bfloat16 [32768, 4096], P('row', 'col'), may hold values from -0.0625 to 0.0625
- rhs0: bfloat16 [65536, 128], P(('row', 'col')), may hold values from -6 to 6
- rhs1: bfloat16 [32768, 128], P(('row', 'col')), may hold values from -6 to 6
- rhs2: bfloat16 [16384, 128], P(('row', 'col')), may hold values from -6 to 6
- block_rows0: int32 [16, 64, 16], replicated, may hold values from 0 to 63, all different within a row
- block_rows1: int32 [8, 64, 16], replicated, may hold values from 0 to 63, all different within a row
Outputs:
- solution0: float32 [65536, 128], P(('row', 'col'))
- solution1: float32 [32768, 128], P(('row', 'col'))
- solution2: float32 [16384, 128], P(('row', 'col'))
The draws below stay inside these ranges and needn't reach their ends.
Inputs may be any that keep to these rules, and one draw needn't show every extreme that they name: `block_rows0`: each row of the last dimension lists 16 different block rows. `block_rows1`: each row of the last dimension lists 16 different block rows. `dinv0`: each supernode's block is lower triangular in global order, with a positive diagonal. `dinv1`: each supernode's block is lower triangular in global order, with a positive diagonal. `dinv2`: each supernode's block is lower triangular in global order, with a positive diagonal.
All inputs are finite; a program needn't handle non-finite values.
Results may differ from the reference program's by a relative error of at most 0.0095.
Values may be sent and summed in bfloat16 or wider, within the bound.
No kernel may reach another device: no remote copies, remote signals or barrier semaphores. Data moves between devices by JAX's collectives and lax.ppermute only.
A program may use at most 64 MiB of HBM per device.

```python
import jax
import jax.numpy as jnp
from jax import lax

SNW = 4096
NRHS = 128
MB = 64
KB = 16
GR = 4
NL0 = 16
NL1 = 8
NL2 = 4
NBLK = 64
CD = 512
MC = 8
N_COL = 8


def inverse_blocks(key, salt, count, group):
    key_off, key_diag = jax.random.split(jax.random.fold_in(key, salt))
    stored = jnp.arange(SNW, dtype=jnp.int32)
    rows_each = SNW // group
    global_rows = (stored % rows_each // MB * group + stored // rows_each) * MB + stored % MB
    inner = stored % CD
    global_columns = inner // MC * MB + stored // CD * MC + inner % MC
    below = global_rows[:, None] > global_columns[None, :]
    same = global_rows[:, None] == global_columns[None, :]
    lower = 0.7 * jax.random.normal(key_off, (count, SNW, SNW), jnp.float32)
    diag_values = jax.random.uniform(key_diag, (count, SNW), jnp.float32, 0.7, 1.4)
    lower = lower * (1.0 / SNW ** 0.5)
    values = jnp.where(below[None, :, :], lower, jnp.where(same[None, :, :], diag_values[:, :, None], 0.0))
    return values.reshape(count * SNW, SNW).astype(jnp.bfloat16)


def draw_dinv0(key, part):
    return inverse_blocks(key, 11, NL0, GR)


def draw_dinv1(key, part):
    return inverse_blocks(key, 23, NL1, 2 * GR)


def draw_dinv2(key, part):
    return inverse_blocks(key, 37, NL2, 4 * GR)


def block_levels(key, shape, cuts, low, largest):
    gain = 1.0
    for axis_at, blocks in cuts:
        heights = jax.random.uniform(jax.random.fold_in(jax.random.fold_in(key, 6), axis_at), (blocks,), jnp.float32, low / len(cuts), largest / len(cuts))
        gain = gain * jnp.repeat(jnp.exp(heights), shape[axis_at] // blocks).reshape((-1,) + (1,) * (len(shape) - 1 - axis_at))
    return gain


def distinct(key, rows, count, top, lift):
    sequence = jax.random.permutation(jax.random.fold_in(key, 1), count)
    favour = sequence
    for power in range(3):
        favour = favour * favour // count
    favour = favour * lift // count
    chance = jax.random.randint(jax.random.fold_in(key, 2), (rows, count), 0, 4096) + favour
    sure = jax.random.permutation(jax.random.fold_in(key, 3), rows)[jnp.arange(count) % rows]
    chance = jnp.where(jnp.arange(rows)[:, None] == sure[None, :], 1 << 14, chance)
    merit = chance * count + jnp.arange(count)
    return lax.top_k(merit.astype(jnp.int32), top)[1].astype(jnp.int32)


def gaussian(rng, shape, scale, most, pieces=(), held_as=jnp.bfloat16):
    result = scale * jax.random.normal(rng, shape, jnp.float32)
    if pieces:
        result = result * block_levels(rng, shape, pieces, -0.22, 0.18)
    return jnp.clip(result, -most, most).astype(held_as)


def setup_inputs(seed: int = 0) -> dict:
    streams_of = jax.random.split(jax.random.key(seed), 11)
    dinv0 = draw_dinv0(jax.random.fold_in(streams_of[10], 71), 0)
    dinv1 = draw_dinv1(jax.random.fold_in(streams_of[10], 71), 0)
    dinv2 = draw_dinv2(jax.random.fold_in(streams_of[10], 71), 0)
    offdiag0 = gaussian(streams_of[3], (NL0 * SNW, SNW), (2 * SNW) ** -0.5, 0.0625, ((0, 64), (1, 8)))
    offdiag1 = gaussian(streams_of[4], (NL1 * SNW, SNW), (2 * SNW) ** -0.5, 0.0625, ((0, 64), (1, 8)))
    rhs0 = gaussian(streams_of[5], (NL0 * SNW, NRHS), 1.0, 6.0, ((0, 512),))
    rhs1 = gaussian(streams_of[6], (NL1 * SNW, NRHS), 1.0, 6.0, ((0, 512),))
    rhs2 = gaussian(streams_of[7], (NL2 * SNW, NRHS), 1.0, 6.0, ((0, 512),))
    block_rows0 = distinct(streams_of[8], NL0 * NBLK, NBLK, KB, 4096).reshape((NL0, NBLK, KB))
    block_rows1 = distinct(streams_of[9], NL1 * NBLK, NBLK, KB, 4096).reshape((NL1, NBLK, KB))
    return {"dinv0": dinv0, "dinv1": dinv1, "dinv2": dinv2, "offdiag0": offdiag0, "offdiag1": offdiag1, "rhs0": rhs0, "rhs1": rhs1, "rhs2": rhs2, "block_rows0": block_rows0, "block_rows1": block_rows1}


def row_order(group):
    stored = jnp.arange(SNW, dtype=jnp.int32)
    rows_each = SNW // group
    owner = stored // rows_each
    block = (stored % rows_each) // MB
    return (block * group + owner) * MB + stored % MB


def column_order():
    stored = jnp.arange(SNW, dtype=jnp.int32)
    owner = stored // CD
    inner = stored % CD
    return (inner // MC) * MB + owner * MC + inner % MC


def piece_order(group):
    stored = jnp.arange(SNW, dtype=jnp.int32)
    blocks = SNW // (group * MB)
    unit = stored % MC
    rest = stored // MC
    block = rest % blocks
    rest = rest // blocks
    column_dev = rest % N_COL
    row_dev = rest // N_COL
    return ((block * group + row_dev) * N_COL + column_dev) * MC + unit


def to_global(side, order, count):
    shaped = side.reshape(count, SNW, NRHS)
    return jnp.zeros_like(shaped).at[:, order].set(shaped)


def masked(matrix, listing, rows, columns):
    identity = jnp.arange(NBLK, dtype=jnp.int32)
    listed = jnp.any(listing[None, :, :] == identity[:, None, None], axis=-1)
    keep = listed[rows // MB][:, columns // MB]
    return jnp.where(keep, matrix, jnp.zeros_like(matrix))


def apply_plain(matrix, vector, rows, columns):
    stored_out = jnp.dot(matrix, vector[columns], preferred_element_type=jnp.float32)
    return jnp.zeros((SNW, NRHS), jnp.float32).at[rows].set(stored_out)


def apply_transposed(matrix, vector, rows, columns):
    stored_out = jnp.dot(matrix.T, vector[rows], preferred_element_type=jnp.float32)
    return jnp.zeros((SNW, NRHS), jnp.float32).at[columns].set(stored_out)


def reference(dinv0, dinv1, dinv2, offdiag0, offdiag1, rhs0, rhs1, rhs2, block_rows0, block_rows1):
    groups = (GR, 2 * GR, 4 * GR)
    counts = (NL0, NL1, NL2)
    inverses = (dinv0, dinv1, dinv2)
    couplings = (offdiag0, offdiag1)
    listings = (block_rows0, block_rows1)
    sides = (rhs0, rhs1, rhs2)
    columns = column_order()
    solved = []
    update = None
    for level in range(3):
        rows = row_order(groups[level])
        right = to_global(sides[level], piece_order(groups[level]), counts[level]).astype(jnp.float32)
        if update is not None:
            right = right - update
        residual = right.astype(jnp.bfloat16)
        matrices = inverses[level].reshape(counts[level], SNW, SNW)
        solved_level = lax.map(lambda item: apply_plain(item[0], item[1], rows, columns).astype(jnp.bfloat16), (matrices, residual))
        solved.append(solved_level)
        if level < 2:
            coupled = couplings[level].reshape(counts[level], SNW, SNW)
            terms = lax.map(lambda item: apply_plain(masked(item[0], item[2], rows, columns), item[1], rows, columns), (coupled, solved_level, listings[level]))
            update = terms.reshape(counts[level] // 2, 2, SNW, NRHS).sum(axis=1)
    outputs = [None, None, None]
    carried = None
    for level in (2, 1, 0):
        rows = row_order(groups[level])
        total = solved[level].astype(jnp.float32)
        if carried is not None:
            total = total - carried
        weighted = total.astype(jnp.bfloat16)
        matrices = inverses[level].reshape(counts[level], SNW, SNW)
        answer = lax.map(lambda item: apply_transposed(item[0], item[1], rows, columns), (matrices, weighted))
        outputs[level] = answer[:, piece_order(groups[level])].reshape(counts[level] * SNW, NRHS)
        if level > 0:
            rounded = answer.astype(jnp.bfloat16)
            child_rows = row_order(groups[level - 1])
            parent_for_child = jnp.repeat(rounded, 2, axis=0)
            coupled = couplings[level - 1].reshape(counts[level - 1], SNW, SNW)
            carried = lax.map(lambda item: apply_transposed(masked(item[0], item[2], child_rows, columns), item[1], child_rows, columns), (coupled, parent_for_child, listings[level - 1]))
    return (outputs[0], outputs[1], outputs[2])
```

```python
import jax
import jax.numpy as jnp
from jax import lax
from jax.sharding import PartitionSpec as P

MB = 64
GR = 4


def row_groups(row_devs, group):
    return [[first + r for r in range(group)] for first in range(0, row_devs, group)]


def family_groups(row_devs, col_devs, group):
    return [
        [(first + s * group + r) * col_devs + c for s in range(2) for c in range(col_devs)]
        for first in range(0, row_devs, 2 * group)
        for r in range(group)
    ]


def exchange(slots, axis, groups=None):
    return lax.all_to_all(slots, axis, 0, 0, axis_index_groups=groups, tiled=True)


def share(piece, count, axis, groups=None):
    slots = lax.optimization_barrier(jnp.broadcast_to(piece[None], (count,) + piece.shape))
    return exchange(slots, axis, groups)


def coupling(values, listings, group):
    row_blocks = values.shape[0] // MB
    position = lax.axis_index("row")
    owned = jnp.arange(row_blocks, dtype=jnp.int32) * group + position % group
    listing = lax.dynamic_index_in_dim(listings, position // group, 0, keepdims=False)
    listed = jnp.any(listing[None, :, :] == owned[:, None, None], axis=-1)
    unit_width = values.shape[1] // listed.shape[1]
    keeping = jnp.repeat(jnp.repeat(listed, MB, axis=0), unit_width, axis=1)
    return jnp.where(keeping, values, jnp.zeros_like(values))


def per_device(dinv0, dinv1, dinv2, offdiag0, offdiag1, rhs0, rhs1, rhs2, block_rows0, block_rows1):
    row_devs = lax.axis_size("row")
    col_devs = lax.axis_size("col")
    unit = MB // col_devs
    width = rhs0.shape[1]
    groups = (GR, 2 * GR, 4 * GR)
    inverses = (dinv0, dinv1, dinv2)
    couplings = (coupling(offdiag0, block_rows0, groups[0]), coupling(offdiag1, block_rows1, groups[1]))
    sides = (rhs0, rhs1, rhs2)
    own = [row_groups(row_devs, group) for group in groups]
    family = [family_groups(row_devs, col_devs, group) for group in groups[:2]]

    def column_form(piece, level):
        gathered = share(piece, groups[level], "row", own[level])
        return gathered.transpose(1, 0, 2, 3).reshape(-1, width)

    def apply_plain(matrix, vector):
        return jnp.dot(matrix, vector, preferred_element_type=jnp.float32)

    def apply_transposed(matrix, vector):
        return jnp.einsum("ij,in->jn", matrix, vector, preferred_element_type=jnp.float32)

    def total(slots):
        return jnp.sum(slots.astype(jnp.float32), axis=0)

    solved = []
    residual = rhs0.reshape(-1, unit, width)
    for level in range(3):
        product = apply_plain(inverses[level], column_form(residual, level)).astype(jnp.bfloat16)
        if level == 2:
            shared = share(product, col_devs, "col")
            break
        slots = product.reshape(-1, col_devs, unit, width).transpose(1, 0, 2, 3)
        piece = total(exchange(slots, "col")).astype(jnp.bfloat16)
        solved.append(piece)
        partial_value = apply_plain(couplings[level], column_form(piece, level)).astype(jnp.bfloat16)
        slots = partial_value.reshape(-1, 2, col_devs, unit, width).transpose(1, 2, 0, 3, 4)
        slots = slots.reshape(2 * col_devs, -1, unit, width)
        update = total(exchange(slots, ("row", "col"), family[level]))
        side = sides[level + 1].reshape(-1, unit, width).astype(jnp.float32)
        residual = (side - update).astype(jnp.bfloat16)

    def row_sum(product, level):
        slots = product.astype(jnp.bfloat16).reshape(-1, groups[level], unit, width)
        return total(exchange(slots.transpose(1, 0, 2, 3), "row", own[level]))

    outputs = [None, None, None]
    row_form = total(shared).astype(jnp.bfloat16)
    for level in (2, 1, 0):
        answer = row_sum(apply_transposed(inverses[level], row_form), level)
        outputs[level] = answer.reshape(-1, width)
        if level > 0:
            child = level - 1
            gathered = share(answer.astype(jnp.bfloat16), 2 * col_devs, ("row", "col"), family[child])
            gathered = gathered.reshape(2, col_devs, -1, unit, width).transpose(2, 0, 1, 3, 4)
            carried = row_sum(apply_transposed(couplings[child], gathered.reshape(-1, width)), child)
            weighted = (solved[child].astype(jnp.float32) - carried).astype(jnp.bfloat16)
            gathered = share(weighted, col_devs, "col")
            row_form = gathered.transpose(1, 0, 2, 3).reshape(-1, width)
    return (outputs[0], outputs[1], outputs[2])


def solution(mesh):
    placed = (
        P("row", "col"),
        P("row", "col"),
        P("row", "col"),
        P("row", "col"),
        P("row", "col"),
        P(("row", "col"), None),
        P(("row", "col"), None),
        P(("row", "col"), None),
        P(),
        P(),
    )
    return jax.shard_map(
        per_device,
        mesh=mesh,
        in_specs=placed,
        out_specs=(P(("row", "col"), None), P(("row", "col"), None), P(("row", "col"), None)),
        check_vma=False,
    )
```

```python
import jax
import jax.numpy as jnp
from jax import lax
from jax.sharding import PartitionSpec as P

MB = 64
GR = 4


def row_groups(row_devs, group):
    return [[first + r for r in range(group)] for first in range(0, row_devs, group)]


def family_groups(row_devs, col_devs, group):
    return [
        [(first + s * group + r) * col_devs + c for s in range(2) for c in range(col_devs)]
        for first in range(0, row_devs, 2 * group)
        for r in range(group)
    ]


def exchange(slots, axis, groups=None):
    return lax.all_to_all(slots, axis, 0, 0, axis_index_groups=groups, tiled=True)


def share(piece, count, axis, groups=None):
    slots = lax.optimization_barrier(jnp.broadcast_to(piece[None], (count,) + piece.shape))
    return exchange(slots, axis, groups)


def coupling(values, listings, group):
    row_blocks = values.shape[0] // MB
    position = lax.axis_index("row")
    owned = jnp.arange(row_blocks, dtype=jnp.int32) * group + position % group
    listing = lax.dynamic_index_in_dim(listings, position // group, 0, keepdims=False)
    listed = jnp.any(listing[None, :, :] == owned[:, None, None], axis=-1)
    blocks = listed.shape[1]
    columns = lax.broadcasted_iota(jnp.int32, (blocks, values.shape[1]), 1) // (values.shape[1] // blocks)
    spread = (columns == lax.broadcasted_iota(jnp.int32, columns.shape, 0)).astype(jnp.bfloat16)
    keeping = jnp.dot(listed.astype(jnp.bfloat16), spread, preferred_element_type=jnp.float32) > 0.5
    shaped = values.reshape(row_blocks, MB, -1)
    return jnp.where(keeping[:, None, :], shaped, jnp.zeros_like(shaped)).reshape(values.shape)


def per_device(dinv0, dinv1, dinv2, offdiag0, offdiag1, rhs0, rhs1, rhs2, block_rows0, block_rows1):
    row_devs = lax.axis_size("row")
    col_devs = lax.axis_size("col")
    unit = MB // col_devs
    width = rhs0.shape[1]
    groups = (GR, 2 * GR, 4 * GR)
    inverses = (dinv0, dinv1, dinv2)
    own = [row_groups(row_devs, group) for group in groups]
    family = family_groups(row_devs, col_devs, groups[1])
    half = lax.axis_index("row") // groups[0] % 2

    def apply_plain(matrix, vector):
        return jnp.dot(matrix, vector, preferred_element_type=jnp.float32).astype(jnp.bfloat16)

    def apply_transposed(matrix, vector):
        product = jnp.einsum("ij,in->jn", matrix, vector, preferred_element_type=jnp.float32)
        return product.astype(jnp.bfloat16)

    def total(slots):
        return jnp.sum(slots.astype(jnp.float32), axis=0)

    def row_gather(piece, level):
        return share(piece, groups[level], "row", own[level])

    def flat(gathered):
        return gathered.transpose(1, 0, 2, 3).reshape(-1, width)

    def column_sum(product):
        slots = product.reshape(-1, col_devs, unit, width).transpose(1, 0, 2, 3)
        return total(exchange(slots, "col"))

    def row_sum(product, level):
        slots = product.reshape(-1, groups[level], unit, width).transpose(1, 0, 2, 3)
        return total(exchange(slots, "row", own[level]))

    mine = lax.broadcasted_iota(jnp.int32, (1, 2, 1, 1), 1) == half
    gathered, coupled0, coupled1, side1, side2 = lax.optimization_barrier(
        (
            row_gather(rhs0.reshape(-1, unit, width), 0),
            coupling(offdiag0, block_rows0, groups[0]),
            coupling(offdiag1, block_rows1, groups[1]),
            jnp.where(mine, rhs1.reshape(-1, 1, unit, width).astype(jnp.float32), 0.0),
            rhs2.reshape(-1, unit, width).astype(jnp.float32),
        )
    )
    solved0 = column_sum(apply_plain(dinv0, flat(gathered))).astype(jnp.bfloat16)
    update = column_sum(apply_plain(coupled0, flat(row_gather(solved0, 0))))
    update = update.reshape(-1, 2, unit, width)
    gathered = row_gather((side1 - update).astype(jnp.bfloat16), 1)
    gathered = gathered.reshape(2, groups[0], -1, unit, width)
    residual = total(gathered).astype(jnp.bfloat16)

    solved1 = column_sum(apply_plain(dinv1, flat(residual))).astype(jnp.bfloat16)
    partial_value = apply_plain(coupled1, flat(row_gather(solved1, 1)))
    slots = partial_value.reshape(-1, 2, col_devs, unit, width).transpose(1, 2, 0, 3, 4)
    slots = slots.reshape(2 * col_devs, -1, unit, width)
    update = total(exchange(slots, ("row", "col"), family))
    residual = (side2 - update).astype(jnp.bfloat16)

    shared = share(apply_plain(dinv2, flat(row_gather(residual, 2))), col_devs, "col")
    row_form = total(shared).astype(jnp.bfloat16)
    answer2 = row_sum(apply_transposed(dinv2, row_form), 2)

    gathered = share(answer2.astype(jnp.bfloat16), 2 * col_devs, ("row", "col"), family)
    gathered = gathered.reshape(2, col_devs, -1, unit, width).transpose(2, 0, 1, 3, 4)
    carried = row_sum(apply_transposed(coupled1, gathered.reshape(-1, width)), 1)
    weighted = (solved1.astype(jnp.float32) - carried).astype(jnp.bfloat16)
    product = apply_transposed(dinv1, flat(share(weighted, col_devs, "col")))
    slots = product.reshape(-1, 2, groups[0], unit, width).transpose(2, 0, 1, 3, 4)
    slots = jnp.broadcast_to(slots[None], (2,) + slots.shape).reshape(groups[1], -1, unit, width)
    both = total(exchange(slots, "row", own[1]))
    pairs = both.reshape(-1, 2, unit, width)
    answer1 = jnp.where(half == 0, pairs[:, 0], pairs[:, 1])
    both, answer1 = lax.optimization_barrier((both, answer1))

    child_form = flat(share(both.astype(jnp.bfloat16), col_devs, "col"))
    carried = row_sum(apply_transposed(coupled0, child_form), 0)
    weighted = (solved0.astype(jnp.float32) - carried).astype(jnp.bfloat16)
    answer0 = row_sum(apply_transposed(dinv0, flat(share(weighted, col_devs, "col"))), 0)
    return tuple(answer.reshape(-1, width) for answer in (answer0, answer1, answer2))


def solution(mesh):
    placed = (
        P("row", "col"),
        P("row", "col"),
        P("row", "col"),
        P("row", "col"),
        P("row", "col"),
        P(("row", "col"), None),
        P(("row", "col"), None),
        P(("row", "col"), None),
        P(),
        P(),
    )
    return jax.shard_map(
        per_device,
        mesh=mesh,
        in_specs=placed,
        out_specs=(P(("row", "col"), None), P(("row", "col"), None), P(("row", "col"), None)),
        check_vma=False,
    )
```

```python
import jax
import jax.numpy as jnp
from jax import lax
from jax.experimental import pallas as pl
from jax.experimental.pallas import tpu as pltpu
from jax.sharding import PartitionSpec as P

MB = 64
GR = 4


def row_groups(row_devs, group):
    return [[first + r for r in range(group)] for first in range(0, row_devs, group)]


def family_groups(row_devs, col_devs, group):
    return [
        [(first + s * group + r) * col_devs + c for s in range(2) for c in range(col_devs)]
        for first in range(0, row_devs, 2 * group)
        for r in range(group)
    ]


def exchange(slots, axis, groups=None):
    return lax.all_to_all(slots, axis, 0, 0, axis_index_groups=groups, tiled=True)


def share(piece, count, axis, groups=None):
    slots = lax.optimization_barrier(jnp.broadcast_to(piece[None], (count,) + piece.shape))
    return exchange(slots, axis, groups)


def kept(values, listings, group):
    row_blocks = values.shape[0] // MB
    position = lax.axis_index("row")
    owned = jnp.arange(row_blocks, dtype=jnp.int32) * group + position % group
    listing = lax.dynamic_index_in_dim(listings, position // group, 0, keepdims=False)
    listed = jnp.any(listing[None, :, :] == owned[:, None, None], axis=-1)
    blocks = listed.shape[1]
    columns = lax.broadcasted_iota(jnp.int32, (blocks, values.shape[1]), 1) // (values.shape[1] // blocks)
    spread = (columns == lax.broadcasted_iota(jnp.int32, columns.shape, 0)).astype(jnp.bfloat16)
    return jnp.dot(listed.astype(jnp.bfloat16), spread, preferred_element_type=jnp.float32) > 0.5


def coupling(values, keeping):
    shaped = values.reshape(keeping.shape[0], MB, -1)
    return jnp.where(keeping[:, None, :], shaped, jnp.zeros_like(shaped)).reshape(values.shape)


def coupled_transposed(values_ref, kept_ref, vector_ref, slots_ref, sums_ref):
    step = pl.program_id(0)
    shaped = values_ref[...].reshape(kept_ref.shape[0], MB, -1) * kept_ref[...]
    product = lax.dot_general(
        shaped.reshape(values_ref.shape),
        vector_ref[...],
        (((0,), (0,)), ((), ())),
        preferred_element_type=jnp.float32,
    )
    sums_ref[...] = jnp.where(step == 0, product, sums_ref[...] + product)

    @pl.when(step == pl.num_programs(0) - 1)
    def _():
        blocks, group, unit, width = slots_ref.shape[1], slots_ref.shape[0], slots_ref.shape[2], slots_ref.shape[3]
        sums = sums_ref[...].reshape(blocks, group, unit, width)
        for r in range(group):
            slots_ref[r] = sums[:, r].astype(slots_ref.dtype)


def coupled_slots(values, keeping, vector, group, unit, steps=4):
    rows, columns = values.shape
    width = vector.shape[1]
    blocks = columns // (group * unit)
    held = rows // MB // steps
    return pl.pallas_call(
        coupled_transposed,
        grid=(steps,),
        in_specs=[
            pl.BlockSpec((rows // steps, columns), lambda i: (i, 0)),
            pl.BlockSpec((held, 1, columns), lambda i: (i, 0, 0)),
            pl.BlockSpec((rows // steps, width), lambda i: (i, 0)),
        ],
        out_specs=pl.BlockSpec((group, blocks, unit, width), lambda i: (0, 0, 0, 0)),
        out_shape=jax.ShapeDtypeStruct((group, blocks, unit, width), jnp.bfloat16),
        scratch_shapes=[pltpu.VMEM((columns, width), jnp.float32)],
        name="coupled_transposed",
    )(values, keeping[:, None, :].astype(jnp.bfloat16), vector)


def per_device(dinv0, dinv1, dinv2, offdiag0, offdiag1, rhs0, rhs1, rhs2, block_rows0, block_rows1):
    row_devs = lax.axis_size("row")
    col_devs = lax.axis_size("col")
    unit = MB // col_devs
    width = rhs0.shape[1]
    groups = (GR, 2 * GR, 4 * GR)
    inverses = (dinv0, dinv1, dinv2)
    own = [row_groups(row_devs, group) for group in groups]
    family = family_groups(row_devs, col_devs, groups[1])
    half = lax.axis_index("row") // groups[0] % 2

    def apply_plain(matrix, vector):
        return jnp.dot(matrix, vector, preferred_element_type=jnp.float32).astype(jnp.bfloat16)

    def apply_transposed(matrix, vector):
        product = jnp.einsum("ij,in->jn", matrix, vector, preferred_element_type=jnp.float32)
        return product.astype(jnp.bfloat16)

    def total(slots):
        return jnp.sum(slots.astype(jnp.float32), axis=0)

    def row_gather(piece, level):
        return share(piece, groups[level], "row", own[level])

    def flat(gathered):
        return gathered.transpose(1, 0, 2, 3).reshape(-1, width)

    def column_sum(product):
        slots = product.reshape(-1, col_devs, unit, width).transpose(1, 0, 2, 3)
        return total(exchange(slots, "col"))

    def row_sum(product, level):
        slots = product.reshape(-1, groups[level], unit, width).transpose(1, 0, 2, 3)
        return total(exchange(slots, "row", own[level]))

    mine = lax.broadcasted_iota(jnp.int32, (1, 2, 1, 1), 1) == half
    gathered, kept0, kept1, side1, side2, first = lax.optimization_barrier(
        (
            row_gather(rhs0.reshape(-1, unit, width), 0),
            kept(offdiag0, block_rows0, groups[0]),
            kept(offdiag1, block_rows1, groups[1]),
            jnp.where(mine, rhs1.reshape(-1, 1, unit, width).astype(jnp.float32), 0.0),
            rhs2.reshape(-1, unit, width).astype(jnp.float32),
            half == 0,
        )
    )
    solved0 = column_sum(apply_plain(dinv0, flat(gathered))).astype(jnp.bfloat16)
    gathered, kept0 = lax.optimization_barrier((row_gather(solved0, 0), kept0))
    update = column_sum(apply_plain(coupling(offdiag0, kept0), flat(gathered)))
    update = update.reshape(-1, 2, unit, width)
    gathered = row_gather((side1 - update).astype(jnp.bfloat16), 1)
    gathered = gathered.reshape(2, groups[0], -1, unit, width)
    residual = total(gathered).astype(jnp.bfloat16)

    solved1 = column_sum(apply_plain(dinv1, flat(residual))).astype(jnp.bfloat16)
    gathered, kept1 = lax.optimization_barrier((row_gather(solved1, 1), kept1))
    partial_value = apply_plain(coupling(offdiag1, kept1), flat(gathered))
    slots = partial_value.reshape(-1, 2, col_devs, unit, width).transpose(1, 2, 0, 3, 4)
    slots = slots.reshape(2 * col_devs, -1, unit, width)
    update = total(exchange(slots, ("row", "col"), family))
    residual = (side2 - update).astype(jnp.bfloat16)

    shared = share(apply_plain(dinv2, flat(row_gather(residual, 2))), col_devs, "col")
    row_form = total(shared).astype(jnp.bfloat16)
    answer2 = row_sum(apply_transposed(dinv2, row_form), 2)

    gathered = share(answer2.astype(jnp.bfloat16), 2 * col_devs, ("row", "col"), family)
    gathered, kept1 = lax.optimization_barrier((gathered, kept1))
    gathered = gathered.reshape(2, col_devs, -1, unit, width).transpose(2, 0, 1, 3, 4)
    carried = row_sum(apply_transposed(coupling(offdiag1, kept1), gathered.reshape(-1, width)), 1)
    weighted = (solved1.astype(jnp.float32) - carried).astype(jnp.bfloat16)
    product = apply_transposed(dinv1, flat(share(weighted, col_devs, "col")))
    slots = product.reshape(-1, 2, groups[0], unit, width).transpose(2, 0, 1, 3, 4)
    slots = jnp.broadcast_to(slots[None], (2,) + slots.shape).reshape(groups[1], -1, unit, width)
    both = total(exchange(slots, "row", own[1]))
    pairs = both.reshape(-1, 2, unit, width)
    answer1 = jnp.where(first, pairs[:, 0], pairs[:, 1])
    both, answer1 = lax.optimization_barrier((both, answer1))

    gathered, kept0 = lax.optimization_barrier((share(both.astype(jnp.bfloat16), col_devs, "col"), kept0))
    slots = coupled_slots(offdiag0, kept0, flat(gathered), groups[0], unit)
    carried = total(exchange(slots, "row", own[0]))
    weighted = (solved0.astype(jnp.float32) - carried).astype(jnp.bfloat16)
    answer0 = row_sum(apply_transposed(dinv0, flat(share(weighted, col_devs, "col"))), 0)
    return tuple(answer.reshape(-1, width) for answer in (answer0, answer1, answer2))


def solution(mesh):
    placed = (
        P("row", "col"),
        P("row", "col"),
        P("row", "col"),
        P("row", "col"),
        P("row", "col"),
        P(("row", "col"), None),
        P(("row", "col"), None),
        P(("row", "col"), None),
        P(),
        P(),
    )
    return jax.shard_map(
        per_device,
        mesh=mesh,
        in_specs=placed,
        out_specs=(P(("row", "col"), None), P(("row", "col"), None), P(("row", "col"), None)),
        check_vma=False,
    )
```

```python
import jax
import jax.numpy as jnp
from jax import lax
from jax.experimental import pallas as pl
from jax.experimental.pallas import tpu as pltpu
from jax.sharding import PartitionSpec as P


MB = 64
GR = 4
CORES = 2


def row_groups(row_devs, group):
    return [[first + r for r in range(group)] for first in range(0, row_devs, group)]


def family_groups(row_devs, col_devs, group):
    return [
        [(first + s * group + r) * col_devs + c for s in range(2) for c in range(col_devs)]
        for first in range(0, row_devs, 2 * group)
        for r in range(group)
    ]


def chip_groups(col_devs):
    return [[core + CORES * chip for chip in range(col_devs // CORES)] for core in range(CORES)]


def swap(values):
    middle = values.shape[-1] // 2
    return jnp.concatenate((values[..., middle:], values[..., :middle]), axis=-1)


def exchange(slots, axis, groups=None):
    return lax.all_to_all(slots, axis, 0, 0, axis_index_groups=groups, tiled=True)


def share(piece, count, axis, groups=None):
    slots = lax.optimization_barrier(jnp.broadcast_to(piece[None], (count,) + piece.shape))
    return exchange(slots, axis, groups)


def kept(values, listings, group):
    row_blocks = values.shape[0] // MB
    position = lax.axis_index("row")
    owned = jnp.arange(row_blocks, dtype=jnp.int32) * group + position % group
    listing = lax.dynamic_index_in_dim(listings, position // group, 0, keepdims=False)
    listed = jnp.any(listing[None, :, :] == owned[:, None, None], axis=-1)
    blocks = listed.shape[1]
    columns = lax.broadcasted_iota(jnp.int32, (blocks, values.shape[1]), 1) // (values.shape[1] // blocks)
    spread = (columns == lax.broadcasted_iota(jnp.int32, columns.shape, 0)).astype(jnp.bfloat16)
    return jnp.dot(listed.astype(jnp.bfloat16), spread, preferred_element_type=jnp.float32) > 0.5


def coupling(values, keeping):
    shaped = values.reshape(keeping.shape[0], MB, -1)
    return jnp.where(keeping[:, None, :], shaped, jnp.zeros_like(shaped)).reshape(values.shape)


def duplicate(source_ref, target_ref, held_ref, in_sems, out_sems):
    steps, rows = held_ref.shape[:2]
    loads = [
        pltpu.make_async_copy(source_ref.at[pl.ds(i * rows, rows)], held_ref.at[i], in_sems.at[i])
        for i in range(steps)
    ]
    stores = [
        pltpu.make_async_copy(held_ref.at[i], target_ref.at[pl.ds(i * rows, rows)], out_sems.at[i])
        for i in range(steps)
    ]
    for load in loads:
        load.start()
    for load, store in zip(loads, stores):
        load.wait()
        store.start()
    for store in stores:
        store.wait()


def second_copy(values, steps=4):
    rows, columns = values.shape
    return pl.pallas_call(
        duplicate,
        in_specs=[pl.BlockSpec(memory_space=pl.ANY)],
        out_specs=pl.BlockSpec(memory_space=pl.ANY),
        out_shape=jax.ShapeDtypeStruct(values.shape, values.dtype),
        scratch_shapes=[
            pltpu.VMEM((steps, rows // steps, columns), values.dtype),
            pltpu.SemaphoreType.DMA((steps,)),
            pltpu.SemaphoreType.DMA((steps,)),
        ],
    )(values)


def per_device(dinv0, dinv1, dinv2, offdiag0, offdiag1, rhs0, rhs1, rhs2, block_rows0, block_rows1):
    row_devs = lax.axis_size("row")
    col_devs = lax.axis_size("col")
    unit = MB // col_devs
    width = rhs0.shape[1]
    groups = (GR, 2 * GR, 4 * GR)
    own = [row_groups(row_devs, group) for group in groups]
    family = family_groups(row_devs, col_devs, groups[1])
    half = lax.axis_index("row") // groups[0] % 2
    upper = lax.axis_index("row") // groups[1] % 2
    column = lax.axis_index("col")
    chips = col_devs // CORES
    lanes = lax.broadcasted_iota(jnp.int32, (1, width), 1) // (width // CORES)
    low = lanes == 0

    def plain(matrix, vector):
        return jnp.dot(matrix, vector, preferred_element_type=jnp.float32)

    def transposed(matrix, vector):
        return jnp.einsum("ij,in->jn", matrix, vector, preferred_element_type=jnp.float32)

    def apply_plain(matrix, vector):
        return plain(matrix, vector).astype(jnp.bfloat16)

    def apply_transposed(matrix, vector):
        return transposed(matrix, vector).astype(jnp.bfloat16)

    def total(slots):
        return jnp.sum(slots.astype(jnp.float32), axis=0)

    def row_gather(piece, level):
        return share(piece, groups[level], "row", own[level])

    def flat(gathered):
        return gathered.transpose(1, 0, 2, 3).reshape(-1, width)

    def column_slots(product):
        return product.reshape(-1, col_devs, unit, width).transpose(1, 0, 2, 3)

    def column_sum(product):
        return total(exchange(column_slots(product), "col"))

    def row_sum(product, level):
        slots = product.reshape(-1, groups[level], unit, width).transpose(1, 0, 2, 3)
        return total(exchange(slots, "row", own[level]))

    gathered, kept0, kept1, inverse0, other2 = lax.optimization_barrier(
        (
            row_gather(rhs0.reshape(-1, unit, width), 0),
            kept(offdiag0, block_rows0, groups[0]),
            kept(offdiag1, block_rows1, groups[1]),
            dinv0,
            lax.ppermute(dinv2, "col", [(i, i ^ 1) for i in range(col_devs)]),
        )
    )
    slots, late1, late2, half, upper, column = lax.optimization_barrier(
        (column_slots(apply_plain(inverse0, flat(gathered))), rhs1, rhs2, half, upper, column)
    )
    received = exchange(slots, "col")
    again0 = second_copy(inverse0)
    mine = lax.broadcasted_iota(jnp.int32, (1, 2, 1, 1), 1) == half
    destination = lax.broadcasted_iota(jnp.int32, (1, 2 * col_devs, 1, 1), 1)
    here = destination == upper * col_devs + column
    received, again0, side1, side2, first, near, low, spot = lax.optimization_barrier(
        (
            received,
            again0,
            jnp.where(mine, late1.reshape(-1, 1, unit, width).astype(jnp.float32), 0.0),
            jnp.where(here, late2.reshape(-1, 1, unit, width).astype(jnp.float32), 0.0),
            half == 0,
            lanes == column % CORES,
            low,
            upper * col_devs + column,
        )
    )
    solved0 = total(received).astype(jnp.bfloat16)
    gathered, kept0 = lax.optimization_barrier((row_gather(solved0, 0), kept0))
    update = column_sum(apply_plain(coupling(offdiag0, kept0), flat(gathered)))
    update = update.reshape(-1, 2, unit, width)
    gathered = row_gather((side1 - update).astype(jnp.bfloat16), 1)
    gathered = gathered.reshape(2, groups[0], -1, unit, width)
    residual = total(gathered).astype(jnp.bfloat16)

    solved1 = column_sum(apply_plain(dinv1, flat(residual))).astype(jnp.bfloat16)
    gathered, kept1 = lax.optimization_barrier((row_gather(solved1, 1), kept1))
    partial_value = plain(coupling(offdiag1, kept1), flat(gathered)).reshape(-1, 2 * col_devs, unit, width)
    partial_value = (side2 - partial_value).astype(jnp.bfloat16)
    even, odd = (
        partial_value.reshape(-1, 2, chips, CORES, unit, width)[:, :, :, u].transpose(1, 2, 0, 3, 4)
        for u in range(CORES)
    )
    slots = jnp.stack((jnp.where(low, even, swap(odd)), jnp.where(low, swap(even), odd)), axis=2)
    slots = slots.reshape(2 * col_devs, -1, unit, width)
    residual = total(exchange(slots, ("row", "col"), family)).astype(jnp.bfloat16)

    vector = flat(row_gather(residual, 2))
    turned = swap(vector)
    product = plain(dinv2, jnp.where(near, vector, turned)) + plain(other2, jnp.where(near, turned, vector))
    product = product.astype(jnp.bfloat16)
    tall = product.shape[0] // CORES
    shared = share(jnp.where(low, product[:tall], product[tall:]), chips, "col", chip_groups(col_devs))
    packed = total(shared).astype(jnp.bfloat16)
    turned = swap(packed)
    row_form = jnp.concatenate((jnp.where(low, packed, turned), jnp.where(low, turned, packed)), axis=0)
    product = jnp.where(near, transposed(dinv2, row_form), transposed(other2, row_form))
    pieces2 = row_sum(product.astype(jnp.bfloat16), 2)

    gathered = share(pieces2.astype(jnp.bfloat16), 2 * col_devs, ("row", "col"), family)
    even, odd = (gathered.reshape(2, chips, CORES, -1, unit, width)[:, :, k] for k in range(CORES))
    gathered = jnp.stack((jnp.where(low, even, swap(odd)), jnp.where(low, swap(even), odd)), axis=3)
    gathered = gathered.transpose(2, 0, 1, 3, 4, 5)
    gathered, pieces2 = lax.optimization_barrier((gathered, pieces2))
    own_unit = lax.dynamic_slice_in_dim(
        gathered.reshape(-1, 2 * col_devs, unit, width), spot, 1, 1, allow_negative_indices=False
    )
    own_unit = own_unit.reshape(pieces2.shape).astype(jnp.float32)
    answer2 = jnp.where(near, pieces2, own_unit)
    gathered, kept1, answer2 = lax.optimization_barrier((gathered, kept1, answer2))
    carried = row_sum(apply_transposed(coupling(offdiag1, kept1), gathered.reshape(-1, width)), 1)
    weighted = (solved1.astype(jnp.float32) - carried).astype(jnp.bfloat16)
    product = apply_transposed(dinv1, flat(share(weighted, col_devs, "col")))
    slots = product.reshape(-1, 2, groups[0], unit, width).transpose(2, 0, 1, 3, 4)
    slots = jnp.broadcast_to(slots[None], (2,) + slots.shape).reshape(groups[1], -1, unit, width)
    both = total(exchange(slots, "row", own[1]))
    pairs = both.reshape(-1, 2, unit, width)
    answer1 = jnp.where(first, pairs[:, 0], pairs[:, 1])
    both, answer1 = lax.optimization_barrier((both, answer1))

    gathered, kept0 = lax.optimization_barrier((share(both.astype(jnp.bfloat16), col_devs, "col"), kept0))
    carried = row_sum(apply_transposed(coupling(offdiag0, kept0), flat(gathered)), 0)
    weighted = (solved0.astype(jnp.float32) - carried).astype(jnp.bfloat16)
    answer0 = row_sum(apply_transposed(again0, flat(share(weighted, col_devs, "col"))), 0)
    return tuple(answer.reshape(-1, width) for answer in (answer0, answer1, answer2))


def solution(mesh):
    placed = (
        P("row", "col"),
        P("row", "col"),
        P("row", "col"),
        P("row", "col"),
        P("row", "col"),
        P(("row", "col"), None),
        P(("row", "col"), None),
        P(("row", "col"), None),
        P(),
        P(),
    )
    return jax.shard_map(
        per_device,
        mesh=mesh,
        in_specs=placed,
        out_specs=(P(("row", "col"), None), P(("row", "col"), None), P(("row", "col"), None)),
        check_vma=False,
    )
```

```python
import jax
import jax.numpy as jnp
from jax import lax
from jax.experimental import pallas as pl
from jax.experimental.pallas import tpu as pltpu
from jax.sharding import PartitionSpec as P


MB = 64
GR = 4
CORES = 2


def row_groups(row_devs, group):
    return [[first + r for r in range(group)] for first in range(0, row_devs, group)]


def family_groups(row_devs, col_devs, group):
    return [
        [(first + s * group + r) * col_devs + c for s in range(2) for c in range(col_devs)]
        for first in range(0, row_devs, 2 * group)
        for r in range(group)
    ]


def chip_groups(col_devs):
    return [[core + CORES * chip for chip in range(col_devs // CORES)] for core in range(CORES)]


def swap(values):
    middle = values.shape[-1] // 2
    return jnp.concatenate((values[..., middle:], values[..., :middle]), axis=-1)


def exchange(slots, axis, groups=None):
    return lax.all_to_all(slots, axis, 0, 0, axis_index_groups=groups, tiled=True)


def share(piece, count, axis, groups=None):
    slots = lax.optimization_barrier(jnp.broadcast_to(piece[None], (count,) + piece.shape))
    return exchange(slots, axis, groups)


def kept(values, listings, group):
    row_blocks = values.shape[0] // MB
    position = lax.axis_index("row")
    owned = jnp.arange(row_blocks, dtype=jnp.int32) * group + position % group
    listing = lax.dynamic_index_in_dim(listings, position // group, 0, keepdims=False)
    listed = jnp.any(listing[None, :, :] == owned[:, None, None], axis=-1)
    blocks = listed.shape[1]
    columns = lax.broadcasted_iota(jnp.int32, (blocks, values.shape[1]), 1) // (values.shape[1] // blocks)
    spread = (columns == lax.broadcasted_iota(jnp.int32, columns.shape, 0)).astype(jnp.bfloat16)
    return jnp.dot(listed.astype(jnp.bfloat16), spread, preferred_element_type=jnp.float32) > 0.5


def coupling(values, keeping):
    shaped = values.reshape(keeping.shape[0], MB, -1)
    return jnp.where(keeping[:, None, :], shaped, jnp.zeros_like(shaped)).reshape(values.shape)


def duplicate(source_ref, target_ref, held_ref, in_sems, out_sems):
    steps, rows = held_ref.shape[:2]
    loads = [
        pltpu.make_async_copy(source_ref.at[pl.ds(i * rows, rows)], held_ref.at[i], in_sems.at[i])
        for i in range(steps)
    ]
    stores = [
        pltpu.make_async_copy(held_ref.at[i], target_ref.at[pl.ds(i * rows, rows)], out_sems.at[i])
        for i in range(steps)
    ]
    for load in loads:
        load.start()
    for load, store in zip(loads, stores):
        load.wait()
        store.start()
    for store in stores:
        store.wait()


def second_copy(values, steps=4):
    rows, columns = values.shape
    return pl.pallas_call(
        duplicate,
        in_specs=[pl.BlockSpec(memory_space=pl.ANY)],
        out_specs=pl.BlockSpec(memory_space=pl.ANY),
        out_shape=jax.ShapeDtypeStruct(values.shape, values.dtype),
        scratch_shapes=[
            pltpu.VMEM((steps, rows // steps, columns), values.dtype),
            pltpu.SemaphoreType.DMA((steps,)),
            pltpu.SemaphoreType.DMA((steps,)),
        ],
    )(values)


def per_device(dinv0, dinv1, dinv2, offdiag0, offdiag1, rhs0, rhs1, rhs2, block_rows0, block_rows1):
    row_devs = lax.axis_size("row")
    col_devs = lax.axis_size("col")
    unit = MB // col_devs
    width = rhs0.shape[1]
    groups = (GR, 2 * GR, 4 * GR)
    own = [row_groups(row_devs, group) for group in groups]
    family = family_groups(row_devs, col_devs, groups[1])
    half = lax.axis_index("row") // groups[0] % 2
    upper = lax.axis_index("row") // groups[1] % 2
    column = lax.axis_index("col")
    chips = col_devs // CORES
    lanes = lax.broadcasted_iota(jnp.int32, (1, width), 1) // (width // CORES)
    low = lanes == 0

    def plain(matrix, vector):
        return jnp.dot(matrix, vector, preferred_element_type=jnp.float32)

    def transposed(matrix, vector):
        return jnp.einsum("ij,in->jn", matrix, vector, preferred_element_type=jnp.float32)

    def apply_plain(matrix, vector):
        return plain(matrix, vector).astype(jnp.bfloat16)

    def apply_transposed(matrix, vector):
        return transposed(matrix, vector).astype(jnp.bfloat16)

    def total(slots):
        return jnp.sum(slots.astype(jnp.float32), axis=0)

    def row_gather(piece, level):
        return share(piece, groups[level], "row", own[level])

    def flat(gathered):
        return gathered.transpose(1, 0, 2, 3).reshape(-1, width)

    def column_slots(product):
        return product.reshape(-1, col_devs, unit, width).transpose(1, 0, 2, 3)

    def column_sum(product):
        return total(exchange(column_slots(product), "col"))

    def row_sum(product, level):
        slots = product.reshape(-1, groups[level], unit, width).transpose(1, 0, 2, 3)
        return total(exchange(slots, "row", own[level]))

    gathered, kept0, kept1, inverse0, inverse2, other2 = lax.optimization_barrier(
        (
            row_gather(rhs0.reshape(-1, unit, width), 0),
            kept(offdiag0, block_rows0, groups[0]),
            kept(offdiag1, block_rows1, groups[1]),
            dinv0,
            dinv2,
            lax.ppermute(dinv2, "col", [(i, i ^ 1) for i in range(col_devs)]),
        )
    )
    slots, late1, late2, half, upper, column = lax.optimization_barrier(
        (column_slots(apply_plain(inverse0, flat(gathered))), rhs1, rhs2, half, upper, column)
    )
    received = exchange(slots, "col")
    again0 = second_copy(inverse0)
    mine = lax.broadcasted_iota(jnp.int32, (1, 2, 1, 1), 1) == half
    destination = lax.broadcasted_iota(jnp.int32, (1, 2 * col_devs, 1, 1), 1)
    here = destination == upper * col_devs + column
    received, again0, side1, side2, first, near, low, spot = lax.optimization_barrier(
        (
            received,
            again0,
            jnp.where(mine, late1.reshape(-1, 1, unit, width).astype(jnp.float32), 0.0),
            jnp.where(here, late2.reshape(-1, 1, unit, width).astype(jnp.float32), 0.0),
            half == 0,
            lanes == column % CORES,
            low,
            upper * col_devs + column,
        )
    )
    solved0 = total(received).astype(jnp.bfloat16)
    gathered, kept0 = lax.optimization_barrier((row_gather(solved0, 0), kept0))
    update = column_sum(apply_plain(coupling(offdiag0, kept0), flat(gathered)))
    update = update.reshape(-1, 2, unit, width)
    gathered = row_gather((side1 - update).astype(jnp.bfloat16), 1)
    gathered = gathered.reshape(2, groups[0], -1, unit, width)
    residual = total(gathered).astype(jnp.bfloat16)

    solved1 = column_sum(apply_plain(dinv1, flat(residual))).astype(jnp.bfloat16)
    gathered, kept1 = lax.optimization_barrier((row_gather(solved1, 1), kept1))
    partial_value = plain(coupling(offdiag1, kept1), flat(gathered)).reshape(-1, 2 * col_devs, unit, width)
    partial_value = (side2 - partial_value).astype(jnp.bfloat16)
    even, odd = (
        partial_value.reshape(-1, 2, chips, CORES, unit, width)[:, :, :, u].transpose(1, 2, 0, 3, 4)
        for u in range(CORES)
    )
    slots = jnp.stack((jnp.where(low, even, swap(odd)), jnp.where(low, swap(even), odd)), axis=2)
    slots = slots.reshape(2 * col_devs, -1, unit, width)
    residual = total(exchange(slots, ("row", "col"), family)).astype(jnp.bfloat16)

    vector = flat(row_gather(residual, 2))
    turned = swap(vector)
    product = plain(inverse2, jnp.where(near, vector, turned)) + plain(other2, jnp.where(near, turned, vector))
    product = product.astype(jnp.bfloat16)
    tall = product.shape[0] // CORES
    shared = share(jnp.where(low, product[:tall], product[tall:]), chips, "col", chip_groups(col_devs))
    packed = total(shared).astype(jnp.bfloat16)
    turned = swap(packed)
    row_form = jnp.concatenate((jnp.where(low, packed, turned), jnp.where(low, turned, packed)), axis=0)
    product = jnp.where(near, transposed(inverse2, row_form), transposed(other2, row_form))
    pieces2 = row_sum(product.astype(jnp.bfloat16), 2)

    gathered = share(pieces2.astype(jnp.bfloat16), 2 * col_devs, ("row", "col"), family)
    even, odd = (gathered.reshape(2, chips, CORES, -1, unit, width)[:, :, k] for k in range(CORES))
    gathered = jnp.stack((jnp.where(low, even, swap(odd)), jnp.where(low, swap(even), odd)), axis=3)
    gathered = gathered.transpose(2, 0, 1, 3, 4, 5)
    gathered, pieces2 = lax.optimization_barrier((gathered, pieces2))
    own_unit = lax.dynamic_slice_in_dim(
        gathered.reshape(-1, 2 * col_devs, unit, width), spot, 1, 1, allow_negative_indices=False
    )
    own_unit = own_unit.reshape(pieces2.shape).astype(jnp.float32)
    gathered, kept1, own_unit = lax.optimization_barrier((gathered, kept1, own_unit))
    carried = row_sum(apply_transposed(coupling(offdiag1, kept1), gathered.reshape(-1, width)), 1)
    weighted = (solved1.astype(jnp.float32) - carried).astype(jnp.bfloat16)
    product = apply_transposed(dinv1, flat(share(weighted, col_devs, "col")))
    slots = product.reshape(-1, 2, groups[0], unit, width).transpose(2, 0, 1, 3, 4)
    slots = jnp.broadcast_to(slots[None], (2,) + slots.shape).reshape(groups[1], -1, unit, width)
    both = total(exchange(slots, "row", own[1]))
    pairs = both.reshape(-1, 2, unit, width)
    gathered = share(both.astype(jnp.bfloat16), col_devs, "col")
    pairs, near, pieces2, own_unit = lax.optimization_barrier((pairs, near, pieces2, own_unit))
    answer1 = jnp.where(first, pairs[:, 0], pairs[:, 1])
    answer2 = jnp.where(near, pieces2, own_unit)
    gathered, kept0, answer1, answer2 = lax.optimization_barrier((gathered, kept0, answer1, answer2))
    carried = row_sum(apply_transposed(coupling(offdiag0, kept0), flat(gathered)), 0)
    weighted = (solved0.astype(jnp.float32) - carried).astype(jnp.bfloat16)
    answer0 = row_sum(apply_transposed(again0, flat(share(weighted, col_devs, "col"))), 0)
    return tuple(answer.reshape(-1, width) for answer in (answer0, answer1, answer2))


def solution(mesh):
    placed = (
        P("row", "col"),
        P("row", "col"),
        P("row", "col"),
        P("row", "col"),
        P("row", "col"),
        P(("row", "col"), None),
        P(("row", "col"), None),
        P(("row", "col"), None),
        P(),
        P(),
    )
    return jax.shard_map(
        per_device,
        mesh=mesh,
        in_specs=placed,
        out_specs=(P(("row", "col"), None), P(("row", "col"), None), P(("row", "col"), None)),
        check_vma=False,
    )
```

```python
import jax
import jax.numpy as jnp
from jax import lax
from jax.experimental import pallas as pl
from jax.experimental.pallas import tpu as pltpu
from jax.sharding import PartitionSpec as P


MB = 64
GR = 4
CORES = 2


def row_groups(row_devs, group):
    return [[first + r for r in range(group)] for first in range(0, row_devs, group)]


def family_groups(row_devs, col_devs, group):
    return [
        [(first + s * group + r) * col_devs + c for s in range(2) for c in range(col_devs)]
        for first in range(0, row_devs, 2 * group)
        for r in range(group)
    ]


def chip_groups(col_devs):
    return [[core + CORES * chip for chip in range(col_devs // CORES)] for core in range(CORES)]


def swap(values):
    middle = values.shape[-1] // 2
    return jnp.concatenate((values[..., middle:], values[..., :middle]), axis=-1)


def exchange(slots, axis, groups=None):
    return lax.all_to_all(slots, axis, 0, 0, axis_index_groups=groups, tiled=True)


def share(piece, count, axis, groups=None):
    slots = lax.optimization_barrier(jnp.broadcast_to(piece[None], (count,) + piece.shape))
    return exchange(slots, axis, groups)


def kept(values, listings, group):
    row_blocks = values.shape[0] // MB
    position = lax.axis_index("row")
    owned = jnp.arange(row_blocks, dtype=jnp.int32) * group + position % group
    listing = lax.dynamic_index_in_dim(listings, position // group, 0, keepdims=False)
    listed = jnp.any(listing[None, :, :] == owned[:, None, None], axis=-1)
    blocks = listed.shape[1]
    columns = lax.broadcasted_iota(jnp.int32, (blocks, values.shape[1]), 1) // (values.shape[1] // blocks)
    spread = (columns == lax.broadcasted_iota(jnp.int32, columns.shape, 0)).astype(jnp.bfloat16)
    return jnp.dot(listed.astype(jnp.bfloat16), spread, preferred_element_type=jnp.float32) > 0.5


def coupling(values, keeping):
    shaped = values.reshape(keeping.shape[0], MB, -1)
    return jnp.where(keeping[:, None, :], shaped, jnp.zeros_like(shaped)).reshape(values.shape)


def duplicate(source_ref, target_ref, held_ref, in_sems, out_sems):
    steps, rows = held_ref.shape[:2]
    loads = [
        pltpu.make_async_copy(source_ref.at[pl.ds(i * rows, rows)], held_ref.at[i], in_sems.at[i])
        for i in range(steps)
    ]
    stores = [
        pltpu.make_async_copy(held_ref.at[i], target_ref.at[pl.ds(i * rows, rows)], out_sems.at[i])
        for i in range(steps)
    ]
    for load in loads:
        load.start()
    for load, store in zip(loads, stores):
        load.wait()
        store.start()
    for store in stores:
        store.wait()


def second_copy(values, steps=4):
    rows, columns = values.shape
    return pl.pallas_call(
        duplicate,
        in_specs=[pl.BlockSpec(memory_space=pl.ANY)],
        out_specs=pl.BlockSpec(memory_space=pl.ANY),
        out_shape=jax.ShapeDtypeStruct(values.shape, values.dtype),
        scratch_shapes=[
            pltpu.VMEM((steps, rows // steps, columns), values.dtype),
            pltpu.SemaphoreType.DMA((steps,)),
            pltpu.SemaphoreType.DMA((steps,)),
        ],
    )(values)


def per_device(dinv0, dinv1, dinv2, offdiag0, offdiag1, rhs0, rhs1, rhs2, block_rows0, block_rows1):
    row_devs = lax.axis_size("row")
    col_devs = lax.axis_size("col")
    unit = MB // col_devs
    width = rhs0.shape[1]
    groups = (GR, 2 * GR, 4 * GR)
    own = [row_groups(row_devs, group) for group in groups]
    family = family_groups(row_devs, col_devs, groups[1])
    half = lax.axis_index("row") // groups[0] % 2
    upper = lax.axis_index("row") // groups[1] % 2
    column = lax.axis_index("col")
    chips = col_devs // CORES
    lanes = lax.broadcasted_iota(jnp.int32, (1, width), 1) // (width // CORES)
    low = lanes == 0

    def plain(matrix, vector):
        return jnp.dot(matrix, vector, preferred_element_type=jnp.float32)

    def transposed(matrix, vector):
        return jnp.einsum("ij,in->jn", matrix, vector, preferred_element_type=jnp.float32)

    def apply_plain(matrix, vector):
        return plain(matrix, vector).astype(jnp.bfloat16)

    def apply_transposed(matrix, vector):
        return transposed(matrix, vector).astype(jnp.bfloat16)

    def total(slots):
        return jnp.sum(slots.astype(jnp.float32), axis=0)

    def row_gather(piece, level):
        return share(piece, groups[level], "row", own[level])

    def flat(gathered):
        return gathered.transpose(1, 0, 2, 3).reshape(-1, width)

    def column_slots(product):
        return product.reshape(-1, col_devs, unit, width).transpose(1, 0, 2, 3)

    def column_sum(product):
        return total(exchange(column_slots(product), "col"))

    def row_sum(product, level):
        slots = product.reshape(-1, groups[level], unit, width).transpose(1, 0, 2, 3)
        return total(exchange(slots, "row", own[level]))

    gathered, kept0, inverse0, other2 = lax.optimization_barrier(
        (
            row_gather(rhs0.reshape(-1, unit, width), 0),
            kept(offdiag0, block_rows0, groups[0]),
            dinv0,
            lax.ppermute(dinv2, "col", [(i, i ^ 1) for i in range(col_devs)]),
        )
    )
    slots, listing1, late1, late2, half, upper, column = lax.optimization_barrier(
        (column_slots(apply_plain(inverse0, flat(gathered))), block_rows1, rhs1, rhs2, half, upper, column)
    )
    received = exchange(slots, "col")
    again0 = second_copy(inverse0)
    kept1 = kept(offdiag1, listing1, groups[1])
    mine = lax.broadcasted_iota(jnp.int32, (1, 2, 1, 1), 1) == half
    destination = lax.broadcasted_iota(jnp.int32, (1, 2 * col_devs, 1, 1), 1)
    here = destination == upper * col_devs + column
    received, again0, kept1, side1, side2, first, near, low, spot = lax.optimization_barrier(
        (
            received,
            again0,
            kept1,
            jnp.where(mine, late1.reshape(-1, 1, unit, width).astype(jnp.float32), 0.0),
            jnp.where(here, late2.reshape(-1, 1, unit, width).astype(jnp.float32), 0.0),
            half == 0,
            lanes == column % CORES,
            low,
            upper * col_devs + column,
        )
    )
    solved0 = total(received).astype(jnp.bfloat16)
    gathered, kept0 = lax.optimization_barrier((row_gather(solved0, 0), kept0))
    update = column_sum(apply_plain(coupling(offdiag0, kept0), flat(gathered)))
    update = update.reshape(-1, 2, unit, width)
    gathered = row_gather((side1 - update).astype(jnp.bfloat16), 1)
    gathered = gathered.reshape(2, groups[0], -1, unit, width)
    residual = total(gathered).astype(jnp.bfloat16)

    solved1 = column_sum(apply_plain(dinv1, flat(residual))).astype(jnp.bfloat16)
    gathered, kept1 = lax.optimization_barrier((row_gather(solved1, 1), kept1))
    partial_value = plain(coupling(offdiag1, kept1), flat(gathered)).reshape(-1, 2 * col_devs, unit, width)
    partial_value = (side2 - partial_value).astype(jnp.bfloat16)
    even, odd = (
        partial_value.reshape(-1, 2, chips, CORES, unit, width)[:, :, :, u].transpose(1, 2, 0, 3, 4)
        for u in range(CORES)
    )
    slots = jnp.stack((jnp.where(low, even, swap(odd)), jnp.where(low, swap(even), odd)), axis=2)
    slots = slots.reshape(2 * col_devs, -1, unit, width)
    residual = total(exchange(slots, ("row", "col"), family)).astype(jnp.bfloat16)

    vector = flat(row_gather(residual, 2))
    turned = swap(vector)
    product = plain(dinv2, jnp.where(near, vector, turned)) + plain(other2, jnp.where(near, turned, vector))
    product = product.astype(jnp.bfloat16)
    tall = product.shape[0] // CORES
    shared = share(jnp.where(low, product[:tall], product[tall:]), chips, "col", chip_groups(col_devs))
    packed = total(shared).astype(jnp.bfloat16)
    turned = swap(packed)
    row_form = jnp.concatenate((jnp.where(low, packed, turned), jnp.where(low, turned, packed)), axis=0)
    product = jnp.where(near, transposed(dinv2, row_form), transposed(other2, row_form))
    pieces2 = row_sum(product.astype(jnp.bfloat16), 2)

    gathered = share(pieces2.astype(jnp.bfloat16), 2 * col_devs, ("row", "col"), family)
    even, odd = (gathered.reshape(2, chips, CORES, -1, unit, width)[:, :, k] for k in range(CORES))
    gathered = jnp.stack((jnp.where(low, even, swap(odd)), jnp.where(low, swap(even), odd)), axis=3)
    gathered = gathered.transpose(2, 0, 1, 3, 4, 5)
    gathered, pieces2 = lax.optimization_barrier((gathered, pieces2))
    own_unit = lax.dynamic_slice_in_dim(
        gathered.reshape(-1, 2 * col_devs, unit, width), spot, 1, 1, allow_negative_indices=False
    )
    own_unit = own_unit.reshape(pieces2.shape).astype(jnp.float32)
    answer2 = jnp.where(near, pieces2, own_unit)
    gathered, kept1, answer2 = lax.optimization_barrier((gathered, kept1, answer2))
    carried = row_sum(apply_transposed(coupling(offdiag1, kept1), gathered.reshape(-1, width)), 1)
    weighted = (solved1.astype(jnp.float32) - carried).astype(jnp.bfloat16)
    product = apply_transposed(dinv1, flat(share(weighted, col_devs, "col")))
    slots = product.reshape(-1, 2, groups[0], unit, width).transpose(2, 0, 1, 3, 4)
    slots = jnp.broadcast_to(slots[None], (2,) + slots.shape).reshape(groups[1], -1, unit, width)
    both = total(exchange(slots, "row", own[1]))
    pairs = both.reshape(-1, 2, unit, width)
    answer1 = jnp.where(first, pairs[:, 0], pairs[:, 1])
    both, answer1 = lax.optimization_barrier((both, answer1))

    gathered, kept0 = lax.optimization_barrier((share(both.astype(jnp.bfloat16), col_devs, "col"), kept0))
    carried = row_sum(apply_transposed(coupling(offdiag0, kept0), flat(gathered)), 0)
    weighted = (solved0.astype(jnp.float32) - carried).astype(jnp.bfloat16)
    answer0 = row_sum(apply_transposed(again0, flat(share(weighted, col_devs, "col"))), 0)
    return tuple(answer.reshape(-1, width) for answer in (answer0, answer1, answer2))


def solution(mesh):
    placed = (
        P("row", "col"),
        P("row", "col"),
        P("row", "col"),
        P("row", "col"),
        P("row", "col"),
        P(("row", "col"), None),
        P(("row", "col"), None),
        P(("row", "col"), None),
        P(),
        P(),
    )
    return jax.shard_map(
        per_device,
        mesh=mesh,
        in_specs=placed,
        out_specs=(P(("row", "col"), None), P(("row", "col"), None), P(("row", "col"), None)),
        check_vma=False,
    )
```
